32 devices in a mesh: dx: 2 (over x), dy: 16 (over z, y, core).
Axes of the slice: x: 2, y: 2, z: 4, core: 2. Of those that a mesh axis runs over, the one named last changes fastest.
Arguments:
- seg_mid: float32 [2, 16, 3, 4096], P('dx', 'dy'), may hold values from 0 to 1
- seg_line: float32 [2, 16, 3, 4096], P('dx', 'dy'), may hold values from -0.3 to 0.3
- seg_burgers: float32 [2, 16, 3, 4096], P('dx', 'dy'), may hold values from -5 to 5
- seg_cell: int32 [2, 16, 4096], P('dx', 'dy'), may hold values from 0 to 71, as said below
- seg_node: int32 [2, 16, 2, 4096], P('dx', 'dy'), may hold values from 0 to 4607, as said below
- ghost_list: int32 [2, 16, 8, 2], P('dx', 'dy'), may hold values from 0 to 31
- ghost_count: int32 [2, 16, 8], P('dx', 'dy'), may hold values from 1 to 2
- pair_list: int32 [2, 16, 32, 12], P('dx', 'dy'), may hold values from 0 to 47, as said below
- pair_count: int32 [2, 16, 32], P('dx', 'dy'), may hold values from 1 to 12
Outputs:
- node_force: float32 [2, 16, 3, 512], P('dx', 'dy')
- cell_moments: float32 [315, 256], P(None, ('dx', 'dy'))
The draws below stay inside these ranges and needn't reach their ends.
Inputs may be any that keep to these rules, and one draw needn't show every extreme that they name: `seg_node`: each entry is d * 512 + m with m a node of the domain at offset (a, b) from the segment's domain, d = 3 (a + 1) + (b + 1), a and b in -1, 0, 1; d = 4 is the domain itself. `seg_cell`: each entry is d * 8 + c with c a cell owned by the domain at offset (a, b) from the segment's domain, d = 3 (a + 1) + (b + 1), a and b in -1, 0, 1; d = 4 is the domain itself. `pair_list`: the entries of one tile's list are distinct.
All inputs are finite; a program needn't handle non-finite values.
Results may differ from the reference program's by a relative error of at most 0.0003.
Values sent between devices are 32-bit elements; how exact they have to be, the bound alone decides.
No kernel may reach another device: no remote copies, remote signals or barrier semaphores. Data moves between devices by JAX's collectives and lax.ppermute only.
A program may use at most 64 MiB of HBM per device.

```python
import jax
import jax.numpy as jnp
import numpy as np
from jax import lax

TILE = 128
TILES = 32
GHOST = 2
NP = 12
NODE_DEV = 512
CELL_DEV = 8
COMPONENTS = 315
SEG_DEV = 4096
POOL = 48
CELLS = 256
N_DX = 2
N_DY = 16


def draw_seg_node(key, part):
    stay_key, other_key, local_key = jax.random.split(jax.random.fold_in(key, 11), 3)
    shape = (N_DX, N_DY, 2, TILES * TILE)
    staying = jax.random.randint(stay_key, shape, 0, 2)
    elsewhere = jax.random.randint(other_key, shape, 0, 8)
    elsewhere = elsewhere + (elsewhere >= 4).astype(jnp.int32)
    direction = jnp.where(staying == 1, 4, elsewhere)
    local_node = jax.random.randint(local_key, shape, 0, NODE_DEV)
    return (direction * NODE_DEV + local_node).astype(jnp.int32)


def draw_seg_cell(key, part):
    stay_key, other_key, local_key = jax.random.split(jax.random.fold_in(key, 37), 3)
    shape = (N_DX, N_DY, TILES * TILE)
    staying = jax.random.randint(stay_key, shape, 0, 2)
    elsewhere = jax.random.randint(other_key, shape, 0, 8)
    elsewhere = elsewhere + (elsewhere >= 4).astype(jnp.int32)
    direction = jnp.where(staying == 1, 4, elsewhere)
    local_cell = jax.random.randint(local_key, shape, 0, CELL_DEV)
    return (direction * CELL_DEV + local_cell).astype(jnp.int32)


def draw_pair_list(key, part):
    pool_size = TILES + 8 * GHOST
    scores = jax.random.randint(jax.random.fold_in(key, 23), (N_DX, N_DY, TILES, pool_size), 0, 1 << 20)
    scores = scores * pool_size + jnp.arange(pool_size, dtype=jnp.int32)
    ranking = jnp.argsort(scores, axis=-1)
    return ranking[..., :NP].astype(jnp.int32)


def touch_ends(result, rng, smallest, top_value):
    shape = result.shape
    index_at = [jax.random.randint(jax.random.fold_in(rng, axis), (), 0, shape[axis]) for axis in range(len(shape))]
    result = result.at[tuple(index_at)].set(smallest)
    longest = shape.index(max(shape))
    index_at[longest] = (index_at[longest] + 1) % shape[longest]
    return result.at[tuple(index_at)].set(top_value)


def block_scale(key, dims, cuts, least, largest):
    factor_of, own = 1.0, jax.random.fold_in(key, 6)
    for dim, blocks in cuts:
        steps = jnp.exp(jax.random.uniform(jax.random.fold_in(own, dim), (blocks,), jnp.float32, least / len(cuts), largest / len(cuts)))
        factor_of = factor_of * jnp.repeat(steps, dims[dim] // blocks).reshape([-1 if axis == dim else 1 for axis in range(len(dims))])
    return factor_of


def normal_values(key, extent, width, bound, pieces=(), kind=jnp.bfloat16):
    values = width * jax.random.normal(key, extent, jnp.float32)
    if pieces:
        values = values * block_scale(key, extent, pieces, -0.22, 0.18)
    return jnp.clip(values, -bound, bound).astype(kind)


def setup_inputs(seed: int = 0) -> dict:
    streams_of = jax.random.split(jax.random.key(seed), 10)
    seg_mid = jnp.clip(1.0 * jax.random.uniform(streams_of[0], (N_DX, N_DY, 3, SEG_DEV), jnp.float32) ** block_scale(streams_of[0], (N_DX, N_DY, 3, SEG_DEV), ((0, 2), (1, 16)), -0.2, 0.2), 0.0, 1.0)
    seg_line = normal_values(streams_of[1], (N_DX, N_DY, 3, SEG_DEV), 0.05, 0.3, ((0, 2), (1, 16)), jnp.float32)
    seg_burgers = normal_values(streams_of[2], (N_DX, N_DY, 3, SEG_DEV), 1.0, 5.0, ((0, 2), (1, 16)), jnp.float32)
    seg_cell = draw_seg_cell(jax.random.fold_in(streams_of[9], 71), 0)
    seg_node = draw_seg_node(jax.random.fold_in(streams_of[9], 71), 0)
    ghost_list = touch_ends(jax.random.randint(streams_of[5], (N_DX, N_DY, 8, GHOST), 0, TILES), jax.random.fold_in(streams_of[5], 1), 0, TILES - 1).astype(jnp.int32)
    ghost_count = touch_ends(jax.random.randint(streams_of[6], (N_DX, N_DY, 8), 1, GHOST + 1), jax.random.fold_in(streams_of[6], 1), 1, GHOST).astype(jnp.int32)
    pair_list = draw_pair_list(jax.random.fold_in(streams_of[9], 71), 0)
    pair_count = touch_ends(jax.random.randint(streams_of[8], (N_DX, N_DY, TILES), 1, NP + 1), jax.random.fold_in(streams_of[8], 1), 1, NP).astype(jnp.int32)
    return dict(seg_mid=seg_mid, seg_line=seg_line, seg_burgers=seg_burgers, seg_cell=seg_cell, seg_node=seg_node, ghost_list=ghost_list, ghost_count=ghost_count, pair_list=pair_list, pair_count=pair_count)


core_radius = 0.1
shear_scale = 0.25
neighbour_offsets = ((-1, -1), (-1, 0), (-1, 1), (0, -1), (0, 1), (1, -1), (1, 0), (1, 1))

def exponent_table():
    exponent_rows = []
    for degree in range(5):
        for first_power in range(degree, -1, -1):
            for second in range(degree - first_power, -1, -1):
                exponent_rows.append((first_power, second, degree - first_power - second))
    return np.array(exponent_rows, dtype=np.int32)

def moment_terms(midpoint, line_vector, burgers):
    scaled = 2.0 * (midpoint - 0.5)
    powers = jnp.stack([jnp.ones_like(scaled), scaled, scaled * scaled, scaled ** 3, scaled ** 4], axis=1)
    exponents = exponent_table()
    monomial = powers[0, exponents[:, 0]] * powers[1, exponents[:, 1]] * powers[2, exponents[:, 2]]
    products = (burgers[:, None, :] * line_vector[None, :, :]).reshape(9, -1)
    return (products[:, None, :] * monomial[None, :, :]).reshape(9 * monomial.shape[0], -1)

def pair_stress(field_tiles, source_tiles, valid_weight):
    separation = [field_tiles[component][:, :, None] - source_tiles[component][:, None, :] for component in range(3)]
    line_source = source_tiles[3:6]
    burgers_source = source_tiles[6:9]
    cross_source = [burgers_source[1] * line_source[2] - burgers_source[2] * line_source[1], burgers_source[2] * line_source[0] - burgers_source[0] * line_source[2], burgers_source[0] * line_source[1] - burgers_source[1] * line_source[0]]
    cross_source = [entry_value[:, None, :] for entry_value in cross_source]
    radius_sq = separation[0] ** 2 + separation[1] ** 2 + separation[2] ** 2 + core_radius ** 2
    inverse = 1.0 / jnp.sqrt(radius_sq)
    weight = shear_scale * valid_weight[:, None, None] * inverse / radius_sq
    projection = separation[0] * cross_source[0] + separation[1] * cross_source[1] + separation[2] * cross_source[2]
    diagonal_term = projection * (1.0 + 1.5 * core_radius ** 2 / radius_sq)
    entries = []
    for first_axis, second_axis in ((0, 0), (1, 1), (2, 2), (0, 1), (0, 2), (1, 2)):
        entry_value = separation[first_axis] * cross_source[second_axis] + separation[second_axis] * cross_source[first_axis] - 3.0 * projection * separation[first_axis] * separation[second_axis] / radius_sq
        if first_axis == second_axis:
            entry_value = entry_value + diagonal_term
        entries.append(lax.optimization_barrier(jnp.sum(weight * entry_value, axis=2)))
    return jnp.stack(entries)

def segment_force(stress, own_columns):
    line_vector = own_columns[3:6]
    burgers = own_columns[6:9]
    traction = [stress[0] * burgers[0] + stress[3] * burgers[1] + stress[4] * burgers[2], stress[3] * burgers[0] + stress[1] * burgers[1] + stress[5] * burgers[2], stress[4] * burgers[0] + stress[5] * burgers[1] + stress[2] * burgers[2]]
    return jnp.stack([traction[1] * line_vector[2] - traction[2] * line_vector[1], traction[2] * line_vector[0] - traction[0] * line_vector[2], traction[0] * line_vector[1] - traction[1] * line_vector[0]])

def reference(seg_mid, seg_line, seg_burgers, seg_cell, seg_node, ghost_list, ghost_count, pair_list, pair_count):
    width_x = seg_mid.shape[0]
    width_y = seg_mid.shape[1]
    seg_data = jnp.concatenate([seg_mid, seg_line, seg_burgers], axis=2)
    own_tiles = seg_data.reshape(width_x, width_y, 9, TILES, TILE).transpose(0, 1, 3, 2, 4)
    packets = jax.vmap(jax.vmap(lambda tile_set, chosen: tile_set[chosen]))(own_tiles, ghost_list)
    slot_valid = (jnp.arange(GHOST, dtype=jnp.int32)[None, None, None, :] < ghost_count[..., None]).astype(jnp.float32)
    packets = packets * slot_valid[..., None, None]
    groups = []
    for group_index in range(8):
        first_shift, second_shift = neighbour_offsets[group_index]
        incoming = jnp.roll(packets[:, :, 7 - group_index], shift=(-first_shift, -second_shift), axis=(0, 1))
        offset_rows = jnp.array([first_shift, second_shift, 0, 0, 0, 0, 0, 0, 0], jnp.float32)
        groups.append(incoming + offset_rows[None, None, None, :, None])
    source_pool = jnp.concatenate([own_tiles] + groups, axis=2)
    total_domains = width_x * width_y

    def domain_partial(inputs):
        pool_dev, own_dev, pairs_dev, limit_dev, ends_dev = inputs
        own_columns = own_dev.transpose(1, 0, 2)

        def add_slot(stress_total, slot_index):
            source_tiles = pool_dev[pairs_dev[:, slot_index]].transpose(1, 0, 2)
            valid_weight = (slot_index < limit_dev).astype(jnp.float32)
            return (stress_total + pair_stress(own_columns, source_tiles, valid_weight), None)
        stress_total, unused = lax.scan(add_slot, jnp.zeros((6, TILES, TILE), jnp.float32), jnp.arange(NP, dtype=jnp.int32))
        force = segment_force(stress_total, own_columns).reshape(3, TILES * TILE)
        halves = 0.5 * force.T
        partial_value = jax.ops.segment_sum(jnp.concatenate([halves, halves], axis=0), jnp.concatenate([ends_dev[0], ends_dev[1]]).astype(jnp.int32), num_segments=9 * NODE_DEV)
        return partial_value.reshape(9, NODE_DEV, 3).transpose(0, 2, 1)
    partials = lax.map(domain_partial, (source_pool.reshape(total_domains, POOL, 9, TILE), own_tiles.reshape(total_domains, TILES, 9, TILE), pair_list.reshape(total_domains, TILES, NP), pair_count.reshape(total_domains, TILES), seg_node.reshape(total_domains, 2, TILES * TILE)))
    partials = partials.reshape(width_x, width_y, 9, 3, NODE_DEV)
    node_force = jnp.zeros((width_x, width_y, 3, NODE_DEV), jnp.float32)
    for direction in range(9):
        node_force = node_force + jnp.roll(partials[:, :, direction], shift=(direction // 3 - 1, direction % 3 - 1), axis=(0, 1))

    def cell_partial(inputs):
        mid_dev, line_dev, burgers_dev, cell_dev = inputs
        terms = moment_terms(mid_dev, line_dev, burgers_dev)
        return jax.ops.segment_sum(terms.T, cell_dev.astype(jnp.int32), num_segments=9 * CELL_DEV)
    cell_parts = lax.map(cell_partial, (seg_mid.reshape(total_domains, 3, TILES * TILE), seg_line.reshape(total_domains, 3, TILES * TILE), seg_burgers.reshape(total_domains, 3, TILES * TILE), seg_cell.reshape(total_domains, TILES * TILE)))
    cell_parts = cell_parts.reshape(width_x, width_y, 9, CELL_DEV, COMPONENTS)
    cell_grid = jnp.zeros((width_x, width_y, CELL_DEV, COMPONENTS), jnp.float32)
    for direction in range(9):
        cell_grid = cell_grid + jnp.roll(cell_parts[:, :, direction], shift=(direction // 3 - 1, direction % 3 - 1), axis=(0, 1))
    return (node_force, cell_grid.reshape(CELLS, COMPONENTS).T)
```

```python
import functools

import jax
import jax.numpy as jnp
import numpy as np
from jax import lax
from jax.experimental import pallas as pl
from jax.experimental.pallas import tpu as pltpu
from jax.sharding import PartitionSpec as P

TILE = 128
NODE_DEV = 512
CELL_DEV = 8
core_radius = 0.1
shear_scale = 0.25
neighbour_offsets = ((-1, -1), (-1, 0), (-1, 1), (0, -1), (0, 1), (1, -1), (1, 0), (1, 1))
MONO = 35
MONO_PAD = 40
MOMENT_LANES = 384
UNROLL = 4
NODE_LOW = 256
f32 = jnp.float32
bf16 = jnp.bfloat16


def passed_along(block, axis, distance):
    size = lax.axis_size(axis)
    route = [((i - distance) % size, i) for i in range(size)]
    return lax.ppermute(block, axis, route)


def exponent_table():
    rows = []
    for degree in range(5):
        for first in range(degree, -1, -1):
            for second in range(degree - first, -1, -1):
                rows.append((first, second, degree - first - second))
    table = np.zeros((3, MONO_PAD, TILE), np.float32)
    table[:, :MONO] = np.array(rows, np.float32).T[:, :, None]
    return table


def nt_dot(left, right):
    return lax.dot_general(left, right, (((1,), (1,)), ((), ())), preferred_element_type=f32)


def two_pieces(value):
    high = value.astype(bf16)
    return high, (value - high.astype(f32)).astype(bf16)


def pack_kernel(ghost_list, ghost_count, mid, line, burgers, pool, out_x, out_up, out_down):
    tiles, slots = pool.shape[0], ghost_list.shape[1]
    for t in range(tiles):
        cols = slice(t * TILE, (t + 1) * TILE)
        b, l = burgers[:, cols], line[:, cols]
        pool[t, 0:3] = mid[:, cols] - 0.5
        pool[t, 3:4] = b[1:2] * l[2:3] - b[2:3] * l[1:2]
        pool[t, 4:5] = b[2:3] * l[0:1] - b[0:1] * l[2:3]
        pool[t, 5:6] = b[0:1] * l[1:2] - b[1:2] * l[0:1]
        pool[t, 6:8] = jnp.zeros((2, TILE), f32)
    for k in range(8):
        for g in range(slots):
            valid = jnp.where(g < ghost_count[k], 1.0, 0.0).astype(f32)
            packet = pool[ghost_list[k, g]] * valid
            if k == 3:
                out_down[g] = packet
            elif k == 4:
                out_up[g] = packet
            else:
                out_x[(k if k < 3 else k - 2) * slots + g] = packet


def moment_kernel(exponents, cell, mid, line, burgers, out, total):
    segments = mid.shape[1]
    chunk = 4 * TILE
    total[...] = jnp.zeros(total.shape, f32)

    def step(i, carry):
        start = pl.multiple_of(i * chunk, chunk)
        u = 2.0 * (mid[:, pl.ds(start, chunk)] - 0.5)
        b, l = burgers[:, pl.ds(start, chunk)], line[:, pl.ds(start, chunk)]
        parts = []
        for j in range(4):
            cols = slice(j * TILE, (j + 1) * TILE)
            value = None
            for c in range(3):
                base = u[c : c + 1, cols]
                powers = [base, base * base]
                powers += [powers[1] * base, powers[1] * powers[1]]
                power = jnp.ones((MONO_PAD, TILE), f32)
                for e in range(4):
                    power = jnp.where(exponents[c] == e + 1.0, powers[e], power)
                value = power if value is None else value * power
            parts.append(value)
        monomial = jnp.concatenate(parts, axis=1)
        rows = lax.broadcasted_iota(jnp.int32, (TILE, chunk), 0)
        member = jnp.where(rows == cell[:, pl.ds(start, chunk)], 1.0, 0.0).astype(bf16)
        for beta in range(3):
            for gamma in range(3):
                p = 3 * beta + gamma
                high, low = two_pieces(monomial * (b[beta : beta + 1] * l[gamma : gamma + 1]))
                total[p] += nt_dot(high, member) + nt_dot(low, member)
        return carry

    lax.fori_loop(0, segments // chunk, step, 0)
    joined = jnp.concatenate([total[p] for p in range(9)], axis=0)
    joined = jnp.concatenate([joined, jnp.zeros((MOMENT_LANES - 9 * MONO_PAD, TILE), f32)], axis=0)
    flipped = jnp.concatenate(
        [joined[k * TILE : (k + 1) * TILE].T for k in range(MOMENT_LANES // TILE)], axis=1
    )
    out[...] = flipped[: 9 * CELL_DEV].reshape(9, CELL_DEV, MOMENT_LANES)


def spread_fields(own, spread, tiles):
    def step(t, carry):
        columns = own[t].T
        for c in range(3):
            spread[t, c] = jnp.broadcast_to(columns[:, c : c + 1], (TILE, TILE))
        return carry

    lax.fori_loop(0, tiles, step, 0, unroll=2)


def write_features(block, features, s):
    y = [block[c : c + 1] for c in range(3)]
    g = [shear_scale * block[c + 3 : c + 4] for c in range(3)]
    ys = [shear_scale * v for v in y]
    near = g + [2.0 * y[c] * g[c] for c in range(3)]
    near += [y[a] * g[b] + y[b] * g[a] for a, b in ((0, 1), (0, 2), (1, 2))]
    near = jnp.concatenate(near + [jnp.zeros((7, TILE), f32)], axis=0)
    far = [jnp.full((1, TILE), shear_scale, f32)] + ys
    far += [y[a] * ys[b] for a, b in ((0, 0), (1, 1), (2, 2), (0, 1), (0, 2), (1, 2))]
    far = jnp.concatenate(far + [jnp.zeros((6, TILE), f32)], axis=0)
    for base, value in ((0, near), (1, far)):
        high, low = two_pieces(value)
        rows, cols = base * 32, base * 2 * TILE
        features[s, rows : rows + 16, cols : cols + TILE] = high
        features[s, rows : rows + 16, cols + TILE : cols + 2 * TILE] = high
        features[s, rows + 16 : rows + 32, cols : cols + TILE] = low
        features[s, rows + 16 : rows + 32, cols + TILE : cols + 2 * TILE] = low
        other = (1 - base) * 2 * TILE
        features[s, rows : rows + 32, other : other + 2 * TILE] = jnp.zeros((32, 2 * TILE), bf16)


def add_items(items, count, pool, features, spread, acc):
    def step(i, carry):
        results = []
        for u in range(UNROLL):
            item = items[i * UNROLL + u]
            t, s = lax.shift_right_logical(item, 6), item & 63
            block = pool[s]
            r = [spread[t, c] - block[c : c + 1] for c in range(3)]
            radius_sq = r[0] * r[0] + r[1] * r[1] + (r[2] * r[2] + core_radius**2)
            inverse = lax.rsqrt(radius_sq)
            inverse_sq = inverse * inverse
            near = inverse_sq * inverse
            p = r[0] * block[3:4] + r[1] * block[4:5] + r[2] * block[5:6]
            far = near * inverse_sq * p
            left = jnp.concatenate([*two_pieces(near), *two_pieces(far)], axis=1)
            results.append((t, nt_dot(left, features[s])))
        for t, value in results:
            acc[t] += value
        return carry

    lax.fori_loop(0, (count + UNROLL - 1) // UNROLL, step, 0)


def own_kernel(pair_list, pair_count, pool, acc, ghost_items, own_items, blocks, features, spread):
    tiles, slots = pair_list.shape

    def listing(t, positions):
        own_at, ghost_at = positions
        limit = pair_count[t]
        for n in range(slots):
            s = pair_list[t, n]
            valid = n < limit
            own_items[own_at] = t * 64 + s
            ghost_items[ghost_at + 1] = t * 64 + (s - tiles)
            own_at = own_at + jnp.where(valid & (s < tiles), 1, 0)
            ghost_at = ghost_at + jnp.where(valid & (s >= tiles), 1, 0)
        return own_at, ghost_at

    own_total, ghost_total = lax.fori_loop(0, tiles, listing, (0, 0))
    ghost_items[0] = ghost_total
    for u in range(UNROLL):
        own_items[own_total + u] = tiles

    def prepare(s, carry):
        block = pool[s]
        blocks[s] = block
        write_features(block, features, s)
        acc[s] = jnp.zeros(acc.shape[1:], f32)
        return carry

    lax.fori_loop(0, tiles, prepare, 0, unroll=2)
    blocks[tiles] = jnp.zeros((8, TILE), f32)
    features[tiles] = jnp.zeros(features.shape[1:], bf16)
    spread_fields(pool, spread, tiles)
    add_items(own_items, own_total, blocks, features, spread, acc)


def tile_force(acc_tile, x, b, l):
    flipped = acc_tile.T
    near = flipped[0:16] + flipped[16:32]
    far = flipped[32:48] + flipped[48:64]
    row = lambda block, k: block[k : k + 1]
    x = [row(x, c) for c in range(3)]
    b = [row(b, c) for c in range(3)]
    l = [row(l, c) for c in range(3)]
    g = [row(near, c) for c in range(3)]
    q0 = row(far, 0)
    q = [row(far, 1 + c) for c in range(3)]
    trace = 0.5 * (row(near, 3) + row(near, 4) + row(near, 5))
    diagonal = x[0] * g[0] + x[1] * g[1] + x[2] * g[2] - trace + 1.5 * core_radius**2 * q0
    s = []
    for k, (m, n) in enumerate(((0, 0), (1, 1), (2, 2), (0, 1), (0, 2), (1, 2))):
        value = x[m] * g[n] + x[n] * g[m] - row(near, 3 + k)
        second = x[m] * (x[n] * q0 - q[n]) - x[n] * q[m] + row(far, 4 + k)
        value = value - 3.0 * second
        s.append(value + diagonal if m == n else value)
    traction = [
        s[0] * b[0] + s[3] * b[1] + s[4] * b[2],
        s[3] * b[0] + s[1] * b[1] + s[5] * b[2],
        s[4] * b[0] + s[5] * b[1] + s[2] * b[2],
    ]
    return [
        0.5 * (traction[1] * l[2] - traction[2] * l[1]),
        0.5 * (traction[2] * l[0] - traction[0] * l[2]),
        0.5 * (traction[0] * l[1] - traction[1] * l[0]),
    ]


def ghost_kernel(merged, *refs):
    ghost_list, own, x_in, below, above, acc_in, line, burgers, node, moments = refs[:10]
    outs, (items, blocks, features, spread, acc, force, grid) = refs[10:-7], refs[-7:]
    tiles, slots = own.shape[0], x_in.shape[0] // 6
    ghosts = 8 * slots
    total = ghost_list[0]

    def copy_item(k, carry):
        items[k] = ghost_list[k + 1]
        return carry

    lax.fori_loop(0, total, copy_item, 0)
    for u in range(UNROLL):
        items[total + u] = ghosts
    groups = [(below, 1), (x_in, 4), (above, 1), (below, 0), (above, 0), (below, 2), (x_in, 1), (above, 2)]
    rows = lax.broadcasted_iota(jnp.int32, (8, TILE), 0)
    for q, (source, place) in enumerate(groups):
        a, b = neighbour_offsets[q]
        shift = jnp.where(rows == 0, float(a), jnp.where(rows == 1, float(b), 0.0))
        for g in range(slots):
            block = source[place * slots + g] + shift
            blocks[q * slots + g] = block
            write_features(block, features, q * slots + g)
    blocks[ghosts] = jnp.zeros((8, TILE), f32)
    features[ghosts] = jnp.zeros(features.shape[1:], bf16)
    spread_fields(own, spread, tiles)
    acc[...] = acc_in[...]
    add_items(items, total, blocks, features, spread, acc)

    def finish(t, carry):
        cols = pl.ds(pl.multiple_of(t * TILE, TILE), TILE)
        rows = tile_force(acc[t], own[t], burgers[:, cols], line[:, cols])
        for c in range(3):
            force[c : c + 1, cols] = rows[c]
        return carry

    lax.fori_loop(0, tiles, finish, 0, unroll=4)
    high_count = 9 * NODE_DEV // NODE_LOW
    chunk = 4 * TILE
    grid[...] = jnp.zeros(grid.shape, f32)

    def scatter(i, carry):
        cols = pl.ds(pl.multiple_of(i * chunk, chunk), chunk)
        pieces = []
        for c in range(3):
            rest = force[c : c + 1, cols]
            for k in range(3):
                piece = rest.astype(bf16).astype(f32)
                pieces.append(piece)
                rest = rest - piece
        for end in range(2):
            index = node[end : end + 1, cols]
            high, low = lax.shift_right_logical(index, 8), index & (NODE_LOW - 1)
            mask = lax.broadcasted_iota(jnp.int32, (32, chunk), 0) == high
            left = jnp.concatenate([jnp.where(mask, v, 0.0).astype(bf16) for v in pieces], axis=0)
            lows = lax.broadcasted_iota(jnp.int32, (NODE_LOW, chunk), 0)
            right = jnp.where(lows == low, 1.0, 0.0).astype(bf16)
            grid[...] += nt_dot(left, right)
        return carry

    lax.fori_loop(0, force.shape[1] // chunk, scatter, 0)
    halves = NODE_DEV // NODE_LOW
    sums = []
    for c in range(3):
        base = c * 96
        sums.append(grid[base : base + 32] + grid[base + 32 : base + 64] + grid[base + 64 : base + 96])

    def part(d):
        blocks = []
        for h in range(halves):
            k = d * halves + h
            blocks.append(jnp.concatenate([sums[c][k : k + 1] for c in range(3)] + [jnp.zeros((5, NODE_LOW), f32)], axis=0))
        return jnp.concatenate([moments[d]] + blocks, axis=1)

    for b in range(3):
        low, middle, high = part(b), part(3 + b), part(6 + b)
        outs[0][b] = middle
        if merged:
            outs[1][b] = low + high
        else:
            outs[1][b] = high
            outs[2][b] = low


def on_device(merged, seg_mid, seg_line, seg_burgers, seg_cell, seg_node, ghost_list, ghost_count, pair_list, pair_count):
    mid, line, burgers = seg_mid[0, 0], seg_line[0, 0], seg_burgers[0, 0]
    tiles, slots = mid.shape[1] // TILE, ghost_list.shape[-1]
    pairs = pair_list.shape[-1]
    vmem = pl.BlockSpec(memory_space=pltpu.VMEM)
    smem = pl.BlockSpec(memory_space=pltpu.SMEM)
    shape = jax.ShapeDtypeStruct
    params = pltpu.CompilerParams(vmem_limit_bytes=50 * 2**20)
    pool, out_x, out_up, out_down = pl.pallas_call(
        pack_kernel,
        in_specs=[smem, smem, vmem, vmem, vmem],
        out_specs=[vmem] * 4,
        out_shape=[shape((k, 8, TILE), f32) for k in (tiles, 6 * slots, slots, slots)],
        name="pack",
    )(ghost_list[0, 0], ghost_count[0, 0], mid, line, burgers)
    if merged:
        x_in = passed_along(out_x, "dx", 1)
    else:
        x_in = jnp.concatenate(
            [passed_along(out_x[: 3 * slots], "dx", -1), passed_along(out_x[3 * slots :], "dx", 1)]
        )
    pick = lambda k: x_in[k * slots : (k + 1) * slots]
    below = passed_along(jnp.concatenate([out_up, pick(5), pick(2)]), "dy", 1)
    above = passed_along(jnp.concatenate([out_down, pick(3), pick(0)]), "dy", -1)
    moments = pl.pallas_call(
        moment_kernel,
        in_specs=[vmem] * 5,
        out_specs=vmem,
        out_shape=shape((9, CELL_DEV, MOMENT_LANES), f32),
        scratch_shapes=[pltpu.VMEM((9, MONO_PAD, TILE), f32)],
        compiler_params=params,
        name="moments",
    )(jnp.asarray(exponent_table()), seg_cell[0], mid, line, burgers)
    room = tiles * pairs + 1 + UNROLL
    acc, ghost_items = pl.pallas_call(
        own_kernel,
        in_specs=[smem, smem, vmem],
        out_specs=[vmem, smem],
        out_shape=[shape((tiles, TILE, 64), f32), shape((room,), jnp.int32)],
        scratch_shapes=[
            pltpu.SMEM((room,), jnp.int32),
            pltpu.VMEM((tiles + 1, 8, TILE), f32),
            pltpu.VMEM((tiles + 1, 64, 4 * TILE), bf16),
            pltpu.VMEM((tiles, 3, TILE, TILE), f32),
        ],
        compiler_params=params,
        name="own_pairs",
    )(pair_list[0, 0], pair_count[0, 0], pool)
    width = MOMENT_LANES + NODE_DEV
    parts = pl.pallas_call(
        functools.partial(ghost_kernel, merged),
        in_specs=[smem] + [vmem] * 9,
        out_specs=[vmem] * (2 if merged else 3),
        out_shape=[shape((3, 8, width), f32)] * (2 if merged else 3),
        scratch_shapes=[
            pltpu.SMEM((room,), jnp.int32),
            pltpu.VMEM((8 * slots + 1, 8, TILE), f32),
            pltpu.VMEM((8 * slots + 1, 64, 4 * TILE), bf16),
            pltpu.VMEM((tiles, 3, TILE, TILE), f32),
            pltpu.VMEM((tiles, TILE, 64), f32),
            pltpu.VMEM((3, tiles * TILE), f32),
            pltpu.VMEM((288, NODE_LOW), f32),
        ],
        compiler_params=params,
        name="ghost_pairs",
    )(ghost_items, pool, x_in, below, above, acc, line, burgers, seg_node[0, 0], moments)
    middle = parts[0] + passed_along(parts[1], "dx", 1)
    if not merged:
        middle = middle + passed_along(parts[2], "dx", -1)
    total = middle[1] + passed_along(middle[2], "dy", 1) + passed_along(middle[0], "dy", -1)
    node_force = total[:3, MOMENT_LANES:]
    cells = total[:, : 9 * MONO_PAD].reshape(CELL_DEV, 9, MONO_PAD)[:, :, :MONO]
    return node_force[None, None], cells.reshape(CELL_DEV, 9 * MONO).T


def solution(mesh):
    in_specs = (
        P("dx", "dy", None, None),
        P("dx", "dy", None, None),
        P("dx", "dy", None, None),
        P("dx", "dy", None),
        P("dx", "dy", None, None),
        P("dx", "dy", None, None),
        P("dx", "dy", None),
        P("dx", "dy", None, None),
        P("dx", "dy", None),
    )
    out_specs = (P("dx", "dy", None, None), P(None, ("dx", "dy")))
    merged = mesh.shape["dx"] == 2
    return jax.shard_map(
        functools.partial(on_device, merged), mesh=mesh, in_specs=in_specs, out_specs=out_specs, check_vma=False
    )
```

```python
import functools

import jax
import jax.numpy as jnp
import numpy as np
from jax import lax
from jax.experimental import pallas as pl
from jax.experimental.pallas import tpu as pltpu
from jax.sharding import PartitionSpec as P

TILE = 128
NODE_DEV = 512
CELL_DEV = 8
core_radius = 0.1
shear_scale = 0.25
neighbour_offsets = ((-1, -1), (-1, 0), (-1, 1), (0, -1), (0, 1), (1, -1), (1, 0), (1, 1))
MONO = 35
MONO_PAD = 40
MOMENT_LANES = 384
UNROLL = 8
NODE_LOW = 256
f32 = jnp.float32
bf16 = jnp.bfloat16


def passed_along(block, axis, distance):
    size = lax.axis_size(axis)
    route = [((i - distance) % size, i) for i in range(size)]
    return lax.ppermute(block, axis, route)


def exponent_table():
    rows = []
    for degree in range(5):
        for first in range(degree, -1, -1):
            for second in range(degree - first, -1, -1):
                rows.append((first, second, degree - first - second))
    table = np.zeros((3, MONO_PAD, TILE), np.float32)
    table[:, :MONO] = np.array(rows, np.float32).T[:, :, None]
    return table


def nt_dot(left, right):
    return lax.dot_general(left, right, (((1,), (1,)), ((), ())), preferred_element_type=f32)


def two_pieces(value):
    high = value.astype(bf16)
    return high, (value - high.astype(f32)).astype(bf16)


def cross(b, l):
    return [b[1] * l[2] - b[2] * l[1], b[2] * l[0] - b[0] * l[2], b[0] * l[1] - b[1] * l[0]]


def pack_kernel(ghost_list, ghost_count, mid, line, burgers, out_x, out_up, out_down):
    slots = ghost_list.shape[0]
    for k in range(8):
        for g in range(slots):
            valid = jnp.where(g < ghost_count[0, k], 1.0, 0.0).astype(f32)
            at = pl.ds(ghost_list[g, k], 1)
            rows = [mid[c, at] - 0.5 for c in range(3)]
            rows += cross([burgers[c, at] for c in range(3)], [line[c, at] for c in range(3)])
            packet = jnp.concatenate(rows + [jnp.zeros((2, TILE), f32)], axis=0) * valid
            if k == 3:
                out_down[g] = packet
            elif k == 4:
                out_up[g] = packet
            else:
                out_x[(k if k < 3 else k - 2) * slots + g] = packet


def moment_kernel(exponents, cell, mid, line, burgers, out, total):
    chunks = mid.shape[1] // 4
    total[...] = jnp.zeros(total.shape, f32)
    half = total.shape[0] // 2

    def step(i, carry):
        places = [pl.ds(4 * i + j, 1) for j in range(4)]
        wide = lambda ref, c: jnp.concatenate([ref[c, at] for at in places], axis=1)
        b, l = [wide(burgers, c) for c in range(3)], [wide(line, c) for c in range(3)]
        parts = []
        for at in places:
            value = None
            for c in range(3):
                base = 2.0 * (mid[c, at] - 0.5)
                powers = [base, base * base]
                powers += [powers[1] * base, powers[1] * powers[1]]
                power = jnp.ones((MONO_PAD, TILE), f32)
                for e in range(4):
                    power = jnp.where(exponents[c] == e + 1.0, powers[e], power)
                value = power if value is None else value * power
            parts.append(value)
        monomial = jnp.concatenate(parts, axis=1)
        rows = lax.broadcasted_iota(jnp.int32, (TILE, 4 * TILE), 0)
        cells = jnp.concatenate([cell[at] for at in places], axis=1)
        member = jnp.where(rows == cells, 1.0, 0.0).astype(bf16)
        terms = [monomial * (b[p // 3] * l[p % 3]) for p in range(9)]
        terms = jnp.concatenate(terms + [jnp.zeros((half - 9 * MONO_PAD, 4 * TILE), f32)], axis=0)
        total[...] += nt_dot(jnp.concatenate(two_pieces(terms), axis=0), member)
        return carry

    lax.fori_loop(0, chunks, step, 0)
    joined = total[:half] + total[half:]
    joined = [joined[p * MONO_PAD : p * MONO_PAD + MONO] for p in range(9)]
    joined = jnp.concatenate(joined + [jnp.zeros((MOMENT_LANES - 9 * MONO, TILE), f32)], axis=0)
    flipped = jnp.concatenate(
        [joined[k * TILE : (k + 1) * TILE].T for k in range(MOMENT_LANES // TILE)], axis=1
    )
    out[...] = flipped[: 9 * CELL_DEV].reshape(9, CELL_DEV, MOMENT_LANES)


def prepare_kernel(pair_list, pair_count, mid, items, spread):
    slots, _, tiles = pair_list.shape

    def listing(t, at):
        for n in range(slots):
            items[at + n + 1] = t * 64 + pair_list[n, 0, t]
        return at + pair_count[0, t]

    items[0] = lax.fori_loop(0, tiles, listing, 0, unroll=2)

    def widen(t, carry):
        rows = [mid[c, pl.ds(t, 1)] - 0.5 for c in range(3)]
        columns = jnp.concatenate(rows + [jnp.zeros((5, TILE), f32)], axis=0).T
        for c in range(3):
            spread[t, c] = jnp.broadcast_to(columns[:, c : c + 1], (TILE, TILE))
        return carry

    lax.fori_loop(0, tiles, widen, 0, unroll=4)


def write_features(source, features, s):
    y = [source[c, pl.ds(s, 1)] for c in range(3)]
    g = [shear_scale * source[c + 3, pl.ds(s, 1)] for c in range(3)]
    ys = [shear_scale * v for v in y]
    near = g + [2.0 * y[c] * g[c] for c in range(3)]
    near += [y[a] * g[b] + y[b] * g[a] for a, b in ((0, 1), (0, 2), (1, 2))]
    near = jnp.concatenate(near + [jnp.zeros((7, TILE), f32)], axis=0)
    far = [jnp.full((1, TILE), shear_scale, f32)] + ys
    far += [y[a] * ys[b] for a, b in ((0, 0), (1, 1), (2, 2), (0, 1), (0, 2), (1, 2))]
    far = jnp.concatenate(far + [jnp.zeros((6, TILE), f32)], axis=0)
    for base, value in ((0, near), (1, far)):
        high, low = two_pieces(value)
        rows, cols = base * 32, base * 2 * TILE
        features[s, rows : rows + 16, cols : cols + TILE] = high
        features[s, rows : rows + 16, cols + TILE : cols + 2 * TILE] = high
        features[s, rows + 16 : rows + 32, cols : cols + TILE] = low
        features[s, rows + 16 : rows + 32, cols + TILE : cols + 2 * TILE] = low
        other = (1 - base) * 2 * TILE
        features[s, rows : rows + 32, other : other + 2 * TILE] = jnp.zeros((32, 2 * TILE), bf16)


def add_items(items, count, source, features, spread, acc):
    def step(i, carry):
        results = []
        for u in range(UNROLL):
            item = items[i * UNROLL + u + 1]
            t, s = lax.shift_right_logical(item, 6), item & 63
            y = [source[c, pl.ds(s, 1)] for c in range(6)]
            r = [spread[t, c] - y[c] for c in range(3)]
            radius_sq = r[0] * r[0] + r[1] * r[1] + (r[2] * r[2] + core_radius**2)
            inverse = lax.rsqrt(radius_sq)
            inverse_sq = inverse * inverse
            near = inverse_sq * inverse
            p = r[0] * y[3] + r[1] * y[4] + r[2] * y[5]
            far = near * inverse_sq * p
            left = jnp.concatenate([*two_pieces(near), *two_pieces(far)], axis=1)
            results.append((t, nt_dot(left, features[s])))
        for t, value in results:
            acc[t] += value
        return carry

    lax.fori_loop(0, (count + UNROLL - 1) // UNROLL, step, 0)


def tile_force(acc_tile, x, b, l):
    flipped = acc_tile.T
    near = flipped[0:16] + flipped[16:32]
    far = flipped[32:48] + flipped[48:64]
    row = lambda block, k: block[k : k + 1]
    g = [row(near, c) for c in range(3)]
    q0 = row(far, 0)
    q = [row(far, 1 + c) for c in range(3)]
    trace = 0.5 * (row(near, 3) + row(near, 4) + row(near, 5))
    diagonal = x[0] * g[0] + x[1] * g[1] + x[2] * g[2] - trace + 1.5 * core_radius**2 * q0
    s = []
    for k, (m, n) in enumerate(((0, 0), (1, 1), (2, 2), (0, 1), (0, 2), (1, 2))):
        value = x[m] * g[n] + x[n] * g[m] - row(near, 3 + k)
        second = x[m] * (x[n] * q0 - q[n]) - x[n] * q[m] + row(far, 4 + k)
        value = value - 3.0 * second
        s.append(value + diagonal if m == n else value)
    traction = [
        s[0] * b[0] + s[3] * b[1] + s[4] * b[2],
        s[3] * b[0] + s[1] * b[1] + s[5] * b[2],
        s[4] * b[0] + s[5] * b[1] + s[2] * b[2],
    ]
    return [
        0.5 * (traction[1] * l[2] - traction[2] * l[1]),
        0.5 * (traction[2] * l[0] - traction[0] * l[2]),
        0.5 * (traction[0] * l[1] - traction[1] * l[0]),
    ]


def pair_kernel(merged, *refs):
    item_list, spread, mid, line, burgers, x_in, below, above, node, moments = refs[:10]
    outs, (items, source, features, acc, force, grid) = refs[10:-6], refs[-6:]
    tiles, slots = mid.shape[1], x_in.shape[0] // 6
    pool = tiles + 8 * slots
    total = item_list[0]

    def copy_items(k, carry):
        for u in range(8):
            items[k * 8 + u + 1] = item_list[k * 8 + u + 1]
        return carry

    lax.fori_loop(0, (total + 7) // 8, copy_items, 0)
    for u in range(UNROLL):
        items[total + u + 1] = pool
    for c in range(3):
        source[c, 0:tiles] = mid[c] - 0.5
    product = cross([burgers[c] for c in range(3)], [line[c] for c in range(3)])
    for c in range(3):
        source[c + 3, 0:tiles] = product[c]
    for c in range(6):
        source[c, pool : pool + 1] = jnp.zeros((1, TILE), f32)
    groups = [(below, 1), (x_in, 4), (above, 1), (below, 0), (above, 0), (below, 2), (x_in, 1), (above, 2)]
    for q, (arrived, place) in enumerate(groups):
        shift = neighbour_offsets[q] + (0,) * 4
        for g in range(slots):
            at = tiles + q * slots + g
            for c in range(6):
                source[c, at : at + 1] = arrived[place * slots + g, c : c + 1] + float(shift[c])

    def prepare(s, carry):
        write_features(source, features, s)
        return carry

    lax.fori_loop(0, pool, prepare, 0, unroll=2)
    features[pool] = jnp.zeros(features.shape[1:], bf16)

    def clear(t, carry):
        acc[t] = jnp.zeros(acc.shape[1:], f32)
        return carry

    lax.fori_loop(0, tiles, clear, 0)
    add_items(items, total, source, features, spread, acc)

    def finish(t, carry):
        at = pl.ds(t, 1)
        pick = lambda ref: [ref[c, at] for c in range(3)]
        rows = tile_force(acc[t], pick(source), pick(burgers), pick(line))
        for c in range(3):
            force[c, at] = rows[c]
        return carry

    lax.fori_loop(0, tiles, finish, 0, unroll=4)
    chunk = 4 * TILE
    grid[...] = jnp.zeros(grid.shape, f32)

    def scatter(i, carry):
        pieces = []
        for c in range(3):
            rest = jnp.concatenate([force[c, pl.ds(4 * i + j, 1)] for j in range(4)], axis=1)
            for k in range(3):
                piece = rest.astype(bf16).astype(f32)
                pieces.append(piece)
                rest = rest - piece
        for end in range(2):
            index = node[end : end + 1, pl.ds(pl.multiple_of(i * chunk, chunk), chunk)]
            high, low = lax.shift_right_logical(index, 8), index & (NODE_LOW - 1)
            mask = lax.broadcasted_iota(jnp.int32, (32, chunk), 0) == high
            left = jnp.concatenate([jnp.where(mask, v, 0.0).astype(bf16) for v in pieces], axis=0)
            lows = lax.broadcasted_iota(jnp.int32, (NODE_LOW, chunk), 0)
            right = jnp.where(lows == low, 1.0, 0.0).astype(bf16)
            grid[...] += nt_dot(left, right)
        return carry

    lax.fori_loop(0, tiles // 4, scatter, 0)
    halves = NODE_DEV // NODE_LOW
    sums = []
    for c in range(3):
        base = c * 96
        sums.append(grid[base : base + 32] + grid[base + 32 : base + 64] + grid[base + 64 : base + 96])

    def part(d):
        blocks = []
        for h in range(halves):
            k = d * halves + h
            blocks.append(jnp.concatenate([sums[c][k : k + 1] for c in range(3)] + [jnp.zeros((5, NODE_LOW), f32)], axis=0))
        return jnp.concatenate([moments[d]] + blocks, axis=1)

    for b in range(3):
        low, middle, high = part(b), part(3 + b), part(6 + b)
        outs[0][b] = middle
        if merged:
            outs[1][b] = low + high
        else:
            outs[1][b] = high
            outs[2][b] = low


def finish_kernel(middle, first, second, node_force, cells):
    total = middle[1] + first[...] + second[...]
    cells[...] = total[:, : cells.shape[1]]
    for k in range(NODE_DEV // TILE):
        at = MOMENT_LANES + k * TILE
        node_force[:, k : k + 1] = total[:3, at : at + TILE].reshape(3, 1, TILE)


def on_device(merged, seg_mid, seg_line, seg_burgers, seg_cell, seg_node, ghost_list, ghost_count, pair_list, pair_count):
    tiles, slots = seg_mid.shape[-1] // TILE, ghost_list.shape[-1]
    mid, line, burgers = [v.reshape(3, tiles, TILE) for v in (seg_mid, seg_line, seg_burgers)]
    cell = seg_cell.reshape(tiles, TILE)
    pairs = pair_list.shape[-1]
    plain = pl.BlockSpec()
    vmem = pl.BlockSpec(memory_space=pltpu.VMEM)
    smem = pl.BlockSpec(memory_space=pltpu.SMEM)
    shape = jax.ShapeDtypeStruct
    params = pltpu.CompilerParams(vmem_limit_bytes=32 * 2**20)
    cost = lambda flops: pl.CostEstimate(flops=flops, transcendentals=0, bytes_accessed=0)
    out_x, out_up, out_down = pl.pallas_call(
        pack_kernel,
        in_specs=[smem, smem] + [plain] * 3,
        out_specs=[plain] * 3,
        out_shape=[shape((k, 8, TILE), f32) for k in (6 * slots, slots, slots)],
        compiler_params=params,
        name="pack",
    )(ghost_list[0, 0].T, ghost_count[0], mid, line, burgers)
    if merged:
        x_in = passed_along(out_x, "dx", 1)
    else:
        x_in = jnp.concatenate(
            [passed_along(out_x[: 3 * slots], "dx", -1), passed_along(out_x[3 * slots :], "dx", 1)]
        )
    pick = lambda k: x_in[k * slots : (k + 1) * slots]
    below = passed_along(jnp.concatenate([out_up, pick(5), pick(2)]), "dy", 1)
    above = passed_along(jnp.concatenate([out_down, pick(3), pick(0)]), "dy", -1)
    moments = pl.pallas_call(
        moment_kernel,
        in_specs=[plain] * 5,
        out_specs=plain,
        out_shape=shape((9, CELL_DEV, MOMENT_LANES), f32),
        scratch_shapes=[pltpu.VMEM((736, TILE), f32)],
        compiler_params=params,
        cost_estimate=cost(3 * 10**9),
        name="moments",
    )(jnp.asarray(exponent_table()), cell, mid, line, burgers)
    room = tiles * pairs + 16
    item_list, spread = pl.pallas_call(
        prepare_kernel,
        in_specs=[smem, smem, plain],
        out_specs=[smem, vmem],
        out_shape=[shape((room,), jnp.int32), shape((tiles, 3, TILE, TILE), f32)],
        compiler_params=params,
        cost_estimate=cost(3 * 10**9),
        name="prepare",
    )(pair_list[0].transpose(2, 0, 1), pair_count[0], mid)
    width = MOMENT_LANES + NODE_DEV
    count = 2 if merged else 3
    pool = tiles + 8 * slots
    parts = pl.pallas_call(
        functools.partial(pair_kernel, merged),
        in_specs=[smem, vmem] + [plain] * 8,
        out_specs=[plain] * count,
        out_shape=[shape((3, 8, width), f32)] * count,
        scratch_shapes=[
            pltpu.SMEM((room,), jnp.int32),
            pltpu.VMEM((6, pool + 1, TILE), f32),
            pltpu.VMEM((pool + 1, 64, 4 * TILE), bf16),
            pltpu.VMEM((tiles, TILE, 64), f32),
            pltpu.VMEM((3, tiles, TILE), f32),
            pltpu.VMEM((288, NODE_LOW), f32),
        ],
        compiler_params=params,
        cost_estimate=cost(10**10),
        name="pairs",
    )(item_list, spread, mid, line, burgers, x_in, below, above, seg_node[0, 0], moments)
    middle = parts[0] + passed_along(parts[1], "dx", 1)
    if not merged:
        middle = middle + passed_along(parts[2], "dx", -1)
    node_force, cells = pl.pallas_call(
        finish_kernel,
        in_specs=[plain] * 3,
        out_specs=[plain] * 2,
        out_shape=[shape((3, NODE_DEV // TILE, TILE), f32), shape((CELL_DEV, 9 * MONO), f32)],
        compiler_params=params,
        name="finish",
    )(middle, passed_along(middle[2], "dy", 1), passed_along(middle[0], "dy", -1))
    return node_force.reshape(1, 1, 3, NODE_DEV), cells.T


def solution(mesh):
    in_specs = (
        P("dx", "dy", None, None),
        P("dx", "dy", None, None),
        P("dx", "dy", None, None),
        P("dx", "dy", None),
        P("dx", "dy", None, None),
        P("dx", "dy", None, None),
        P("dx", "dy", None),
        P("dx", "dy", None, None),
        P("dx", "dy", None),
    )
    out_specs = (P("dx", "dy", None, None), P(None, ("dx", "dy")))
    merged = mesh.shape["dx"] == 2
    return jax.shard_map(
        functools.partial(on_device, merged), mesh=mesh, in_specs=in_specs, out_specs=out_specs, check_vma=False
    )
```

```python
import functools

import jax
import jax.numpy as jnp
import numpy as np
from jax import lax
from jax.experimental import pallas as pl
from jax.experimental.pallas import tpu as pltpu
from jax.sharding import PartitionSpec as P

TILE = 128
NODE_DEV = 512
CELL_DEV = 8
core_radius = 0.1
shear_scale = 0.25
neighbour_offsets = ((-1, -1), (-1, 0), (-1, 1), (0, -1), (0, 1), (1, -1), (1, 0), (1, 1))
MONO = 35
MONO_PAD = 40
MOMENT_LANES = 384
UNROLL = 8
NODE_LOW = 256
f32 = jnp.float32
bf16 = jnp.bfloat16


def moved(block, offset):
    width, length = lax.axis_size("dx"), lax.axis_size("dy")
    route = []
    for i in range(width):
        for j in range(length):
            target = (i + offset[0]) % width * length + (j + offset[1]) % length
            route.append((i * length + j, target))
    return lax.ppermute(block, ("dx", "dy"), route)


def packet_plan(merged):
    if merged:
        return [((1, 1), (2, 7)), ((1, -1), (0, 5)), ((1, 0), (1, 6)), ((0, 1), (4,)), ((0, -1), (3,))]
    return [(neighbour_offsets[k], (k,)) for k in range(8)]


def owner_plan(merged):
    plan = [(offset, tuple(k + (k > 3) for k in held)) for offset, held in packet_plan(merged)]
    return [((0, 0), (4,))] + plan


def exponent_table():
    rows = []
    for degree in range(5):
        for first in range(degree, -1, -1):
            for second in range(degree - first, -1, -1):
                rows.append((first, second, degree - first - second))
    table = np.zeros((3, MONO_PAD, TILE), np.float32)
    table[:, :MONO] = np.array(rows, np.float32).T[:, :, None]
    return table


def nt_dot(left, right):
    return lax.dot_general(left, right, (((1,), (1,)), ((), ())), preferred_element_type=f32)


def two_pieces(value):
    high = value.astype(bf16)
    return high, (value - high.astype(f32)).astype(bf16)


def cross(b, l):
    return [b[1] * l[2] - b[2] * l[1], b[2] * l[0] - b[0] * l[2], b[0] * l[1] - b[1] * l[0]]


def pack_kernel(plan, *refs):
    (ghost_list, ghost_count), arrays = refs[:2], refs[2:10]
    packets, copies, (lists, counts, sems) = refs[10:-11], refs[-11:-3], refs[-3:]
    started = [pltpu.make_async_copy(ghost_list, lists, sems.at[8])]
    started += [pltpu.make_async_copy(ghost_count, counts, sems.at[9])]
    started += [pltpu.make_async_copy(a, b, sems.at[k]) for k, (a, b) in enumerate(zip(arrays, copies))]
    for copy in started:
        copy.start()
    for copy in started:
        copy.wait()
    mid, line, burgers = copies[:3]
    slots = lists.shape[0]
    for out, (offset, held) in zip(packets, plan):
        for place, k in enumerate(held):
            for g in range(slots):
                valid = jnp.where(g < counts[0, k], 1.0, 0.0).astype(f32)
                at = pl.ds(lists[g, k], 1)
                rows = [mid[c, at] - 0.5 for c in range(3)]
                rows += cross([burgers[c, at] for c in range(3)], [line[c, at] for c in range(3)])
                packet = jnp.concatenate(rows + [jnp.zeros((2, TILE), f32)], axis=0) * valid
                out[place * slots + g] = packet


def moment_kernel(exponents, cell, mid, line, burgers, out, total):
    chunks = mid.shape[1] // 4
    total[...] = jnp.zeros(total.shape, f32)
    half = total.shape[0] // 2

    def step(i, carry):
        places = [pl.ds(4 * i + j, 1) for j in range(4)]
        wide = lambda ref, c: jnp.concatenate([ref[c, at] for at in places], axis=1)
        b, l = [wide(burgers, c) for c in range(3)], [wide(line, c) for c in range(3)]
        parts = []
        for at in places:
            value = None
            for c in range(3):
                base = 2.0 * (mid[c, at] - 0.5)
                powers = [base, base * base]
                powers += [powers[1] * base, powers[1] * powers[1]]
                power = jnp.ones((MONO_PAD, TILE), f32)
                for e in range(4):
                    power = jnp.where(exponents[c] == e + 1.0, powers[e], power)
                value = power if value is None else value * power
            parts.append(value)
        monomial = jnp.concatenate(parts, axis=1)
        rows = lax.broadcasted_iota(jnp.int32, (TILE, 4 * TILE), 0)
        cells = jnp.concatenate([cell[at] for at in places], axis=1)
        member = jnp.where(rows == cells, 1.0, 0.0).astype(bf16)
        terms = [monomial * (b[p // 3] * l[p % 3]) for p in range(9)]
        terms = jnp.concatenate(terms + [jnp.zeros((half - 9 * MONO_PAD, 4 * TILE), f32)], axis=0)
        total[...] += nt_dot(jnp.concatenate(two_pieces(terms), axis=0), member)
        return carry

    lax.fori_loop(0, chunks, step, 0)
    joined = total[:half] + total[half:]
    joined = [joined[p * MONO_PAD : p * MONO_PAD + MONO] for p in range(9)]
    joined = jnp.concatenate(joined + [jnp.zeros((MOMENT_LANES - 9 * MONO, TILE), f32)], axis=0)
    flipped = jnp.concatenate(
        [joined[k * TILE : (k + 1) * TILE].T for k in range(MOMENT_LANES // TILE)], axis=1
    )
    out[...] = flipped[: 9 * CELL_DEV].reshape(9, CELL_DEV, MOMENT_LANES)


def prepare_kernel(pair_list, pair_count, mid, items, spread):
    slots, _, tiles = pair_list.shape

    def listing(t, at):
        for n in range(slots):
            items[at + n + 1] = t * 64 + pair_list[n, 0, t]
        return at + pair_count[0, t]

    items[0] = lax.fori_loop(0, tiles, listing, 0, unroll=2)

    def widen(t, carry):
        rows = [mid[c, pl.ds(t, 1)] - 0.5 for c in range(3)]
        columns = jnp.concatenate(rows + [jnp.zeros((5, TILE), f32)], axis=0).T
        for c in range(3):
            spread[t, c] = jnp.broadcast_to(columns[:, c : c + 1], (TILE, TILE))
        return carry

    lax.fori_loop(0, tiles, widen, 0, unroll=4)


def write_features(source, features, s):
    y = [source[c, pl.ds(s, 1)] for c in range(3)]
    g = [shear_scale * source[c + 3, pl.ds(s, 1)] for c in range(3)]
    ys = [shear_scale * v for v in y]
    near = g + [2.0 * y[c] * g[c] for c in range(3)]
    near += [y[a] * g[b] + y[b] * g[a] for a, b in ((0, 1), (0, 2), (1, 2))]
    near = jnp.concatenate(near + [jnp.zeros((7, TILE), f32)], axis=0)
    far = [jnp.full((1, TILE), shear_scale, f32)] + ys
    far += [y[a] * ys[b] for a, b in ((0, 0), (1, 1), (2, 2), (0, 1), (0, 2), (1, 2))]
    far = jnp.concatenate(far + [jnp.zeros((6, TILE), f32)], axis=0)
    for base, value in ((0, near), (1, far)):
        high, low = two_pieces(value)
        rows, cols = base * 32, base * 2 * TILE
        features[s, rows : rows + 16, cols : cols + TILE] = high
        features[s, rows : rows + 16, cols + TILE : cols + 2 * TILE] = high
        features[s, rows + 16 : rows + 32, cols : cols + TILE] = low
        features[s, rows + 16 : rows + 32, cols + TILE : cols + 2 * TILE] = low
        other = (1 - base) * 2 * TILE
        features[s, rows : rows + 32, other : other + 2 * TILE] = jnp.zeros((32, 2 * TILE), bf16)


def add_items(items, count, source, features, spread, acc):
    def step(i, carry):
        results = []
        for u in range(UNROLL):
            item = items[i * UNROLL + u + 1]
            t, s = lax.shift_right_logical(item, 6), item & 63
            y = [source[c, pl.ds(s, 1)] for c in range(6)]
            r = [spread[t, c] - y[c] for c in range(3)]
            radius_sq = r[0] * r[0] + r[1] * r[1] + (r[2] * r[2] + core_radius**2)
            inverse = lax.rsqrt(radius_sq)
            inverse_sq = inverse * inverse
            near = inverse_sq * inverse
            p = r[0] * y[3] + r[1] * y[4] + r[2] * y[5]
            far = near * inverse_sq * p
            left = jnp.concatenate([*two_pieces(near), *two_pieces(far)], axis=1)
            results.append((t, nt_dot(left, features[s])))
        for t, value in results:
            acc[t] += value
        return carry

    lax.fori_loop(0, (count + UNROLL - 1) // UNROLL, step, 0)


def tile_force(acc_tile, x, b, l):
    flipped = acc_tile.T
    near = flipped[0:16] + flipped[16:32]
    far = flipped[32:48] + flipped[48:64]
    row = lambda block, k: block[k : k + 1]
    g = [row(near, c) for c in range(3)]
    q0 = row(far, 0)
    q = [row(far, 1 + c) for c in range(3)]
    trace = 0.5 * (row(near, 3) + row(near, 4) + row(near, 5))
    diagonal = x[0] * g[0] + x[1] * g[1] + x[2] * g[2] - trace + 1.5 * core_radius**2 * q0
    s = []
    for k, (m, n) in enumerate(((0, 0), (1, 1), (2, 2), (0, 1), (0, 2), (1, 2))):
        value = x[m] * g[n] + x[n] * g[m] - row(near, 3 + k)
        second = x[m] * (x[n] * q0 - q[n]) - x[n] * q[m] + row(far, 4 + k)
        value = value - 3.0 * second
        s.append(value + diagonal if m == n else value)
    traction = [
        s[0] * b[0] + s[3] * b[1] + s[4] * b[2],
        s[3] * b[0] + s[1] * b[1] + s[5] * b[2],
        s[4] * b[0] + s[5] * b[1] + s[2] * b[2],
    ]
    return [
        0.5 * (traction[1] * l[2] - traction[2] * l[1]),
        0.5 * (traction[2] * l[0] - traction[0] * l[2]),
        0.5 * (traction[0] * l[1] - traction[1] * l[0]),
    ]


def pair_kernel(merged, slots, *refs):
    item_list, spread, mid, line, burgers, node, moments = refs[:7]
    plan, owners = packet_plan(merged), owner_plan(merged)
    arrivals, outs = refs[7 : 7 + len(plan)], refs[7 + len(plan) : -6]
    items, source, features, acc, force, grid = refs[-6:]
    tiles = mid.shape[1]
    pool = tiles + 8 * slots
    total = item_list[0]

    def copy_items(k, carry):
        for u in range(8):
            items[k * 8 + u + 1] = item_list[k * 8 + u + 1]
        return carry

    lax.fori_loop(0, (total + 7) // 8, copy_items, 0)
    for u in range(UNROLL):
        items[total + u + 1] = pool
    for c in range(3):
        source[c, 0:tiles] = mid[c] - 0.5
    product = cross([burgers[c] for c in range(3)], [line[c] for c in range(3)])
    for c in range(3):
        source[c + 3, 0:tiles] = product[c]
    for c in range(6):
        source[c, pool : pool + 1] = jnp.zeros((1, TILE), f32)
    where = {k: (arrived, place) for arrived, (offset, held) in zip(arrivals, plan) for place, k in enumerate(held)}
    for q in range(8):
        arrived, place = where[7 - q]
        shift = neighbour_offsets[q] + (0,) * 4
        for g in range(slots):
            at = tiles + q * slots + g
            for c in range(6):
                source[c, at : at + 1] = arrived[place * slots + g, c : c + 1] + float(shift[c])

    def prepare(s, carry):
        write_features(source, features, s)
        return carry

    lax.fori_loop(0, pool, prepare, 0, unroll=2)
    features[pool] = jnp.zeros(features.shape[1:], bf16)

    def clear(t, carry):
        acc[t] = jnp.zeros(acc.shape[1:], f32)
        return carry

    lax.fori_loop(0, tiles, clear, 0)
    add_items(items, total, source, features, spread, acc)

    def finish(t, carry):
        at = pl.ds(t, 1)
        pick = lambda ref: [ref[c, at] for c in range(3)]
        rows = tile_force(acc[t], pick(source), pick(burgers), pick(line))
        for c in range(3):
            force[c, at] = rows[c]
        return carry

    lax.fori_loop(0, tiles, finish, 0, unroll=4)
    chunk = 4 * TILE
    grid[...] = jnp.zeros(grid.shape, f32)

    def scatter(i, carry):
        pieces = []
        for c in range(3):
            rest = jnp.concatenate([force[c, pl.ds(4 * i + j, 1)] for j in range(4)], axis=1)
            for k in range(3):
                piece = rest.astype(bf16).astype(f32)
                pieces.append(piece)
                rest = rest - piece
        for end in range(2):
            index = node[end : end + 1, pl.ds(pl.multiple_of(i * chunk, chunk), chunk)]
            high, low = lax.shift_right_logical(index, 8), index & (NODE_LOW - 1)
            mask = lax.broadcasted_iota(jnp.int32, (32, chunk), 0) == high
            left = jnp.concatenate([jnp.where(mask, v, 0.0).astype(bf16) for v in pieces], axis=0)
            lows = lax.broadcasted_iota(jnp.int32, (NODE_LOW, chunk), 0)
            right = jnp.where(lows == low, 1.0, 0.0).astype(bf16)
            grid[...] += nt_dot(left, right)
        return carry

    lax.fori_loop(0, tiles // 4, scatter, 0)
    halves = NODE_DEV // NODE_LOW
    sums = []
    for c in range(3):
        base = c * 96
        sums.append(grid[base : base + 32] + grid[base + 32 : base + 64] + grid[base + 64 : base + 96])

    def part(d):
        blocks = []
        for h in range(halves):
            k = d * halves + h
            blocks.append(jnp.concatenate([sums[c][k : k + 1] for c in range(3)] + [jnp.zeros((5, NODE_LOW), f32)], axis=0))
        return jnp.concatenate([moments[d]] + blocks, axis=1)

    for out, (offset, held) in zip(outs, owners):
        value = part(held[0])
        for d in held[1:]:
            value = value + part(d)
        out[...] = value


def finish_kernel(*refs):
    parts, (node_force, cells) = refs[:-2], refs[-2:]
    total = parts[0][...]
    for other in parts[1:]:
        total = total + other[...]
    cells[...] = total[:, : cells.shape[1]]
    for k in range(NODE_DEV // TILE):
        at = MOMENT_LANES + k * TILE
        node_force[:, k : k + 1] = total[:3, at : at + TILE].reshape(3, 1, TILE)


def on_device(merged, seg_mid, seg_line, seg_burgers, seg_cell, seg_node, ghost_list, ghost_count, pair_list, pair_count):
    tiles, slots = seg_mid.shape[-1] // TILE, ghost_list.shape[-1]
    mid, line, burgers = [v.reshape(3, tiles, TILE) for v in (seg_mid, seg_line, seg_burgers)]
    cell = seg_cell.reshape(tiles, TILE)
    exponents = jnp.asarray(exponent_table())
    inputs = (mid, line, burgers, cell, seg_node[0, 0], exponents)
    inputs += (pair_list[0].transpose(2, 0, 1), pair_count[0])
    pairs = pair_list.shape[-1]
    plain = pl.BlockSpec()
    vmem = pl.BlockSpec(memory_space=pltpu.VMEM)
    hbm = pl.BlockSpec(memory_space=pltpu.HBM)
    smem = pl.BlockSpec(memory_space=pltpu.SMEM)
    shape = jax.ShapeDtypeStruct
    params = pltpu.CompilerParams(vmem_limit_bytes=32 * 2**20)
    cost = lambda flops: pl.CostEstimate(flops=flops, transcendentals=0, bytes_accessed=0)
    plan, owners = packet_plan(merged), owner_plan(merged)
    lists, counts = ghost_list[0, 0].T, ghost_count[0]
    results = pl.pallas_call(
        functools.partial(pack_kernel, plan),
        in_specs=[hbm] * 10,
        out_specs=[vmem] * (len(plan) + 8),
        out_shape=[shape((len(held) * slots, 8, TILE), f32) for offset, held in plan]
        + [shape(v.shape, v.dtype) for v in inputs],
        scratch_shapes=[
            pltpu.SMEM(lists.shape, jnp.int32),
            pltpu.SMEM(counts.shape, jnp.int32),
            pltpu.SemaphoreType.DMA((10,)),
        ],
        compiler_params=params,
        name="pack",
    )(*[pltpu.with_memory_space_constraint(v, pltpu.HBM) for v in (lists, counts, *inputs)])
    arrivals = [moved(packet, offset) for packet, (offset, held) in zip(results, plan)]
    mid, line, burgers, cell, node, exponents, pair_rows, pair_limits = results[len(plan) :]
    moments = pl.pallas_call(
        moment_kernel,
        in_specs=[vmem] * 5,
        out_specs=vmem,
        out_shape=shape((9, CELL_DEV, MOMENT_LANES), f32),
        scratch_shapes=[pltpu.VMEM((736, TILE), f32)],
        compiler_params=params,
        cost_estimate=cost(3 * 10**9),
        name="moments",
    )(exponents, cell, mid, line, burgers)
    room = tiles * pairs + 16
    item_list, spread = pl.pallas_call(
        prepare_kernel,
        in_specs=[smem, smem, vmem],
        out_specs=[smem, vmem],
        out_shape=[shape((room,), jnp.int32), shape((tiles, 3, TILE, TILE), f32)],
        compiler_params=params,
        cost_estimate=cost(3 * 10**9),
        name="prepare",
    )(pair_rows, pair_limits, mid)
    width = MOMENT_LANES + NODE_DEV
    pool = tiles + 8 * slots
    parts = pl.pallas_call(
        functools.partial(pair_kernel, merged, slots),
        in_specs=[smem] + [vmem] * (6 + len(plan)),
        out_specs=[vmem] * len(owners),
        out_shape=[shape((8, width), f32)] * len(owners),
        scratch_shapes=[
            pltpu.SMEM((room,), jnp.int32),
            pltpu.VMEM((6, pool + 1, TILE), f32),
            pltpu.VMEM((pool + 1, 64, 4 * TILE), bf16),
            pltpu.VMEM((tiles, TILE, 64), f32),
            pltpu.VMEM((3, tiles, TILE), f32),
            pltpu.VMEM((288, NODE_LOW), f32),
        ],
        compiler_params=params,
        cost_estimate=cost(10**10),
        name="pairs",
    )(item_list, spread, mid, line, burgers, node, moments, *arrivals)
    totals = [parts[0]] + [moved(v, offset) for v, (offset, held) in zip(parts[1:], owners[1:])]
    node_force, cells = pl.pallas_call(
        finish_kernel,
        in_specs=[vmem] * len(totals),
        out_specs=[plain] * 2,
        out_shape=[shape((3, NODE_DEV // TILE, TILE), f32), shape((CELL_DEV, 9 * MONO), f32)],
        compiler_params=params,
        name="finish",
    )(*totals)
    return node_force.reshape(1, 1, 3, NODE_DEV), cells.T


def solution(mesh):
    in_specs = (
        P("dx", "dy", None, None),
        P("dx", "dy", None, None),
        P("dx", "dy", None, None),
        P("dx", "dy", None),
        P("dx", "dy", None, None),
        P("dx", "dy", None, None),
        P("dx", "dy", None),
        P("dx", "dy", None, None),
        P("dx", "dy", None),
    )
    out_specs = (P("dx", "dy", None, None), P(None, ("dx", "dy")))
    merged = mesh.shape["dx"] == 2
    return jax.shard_map(
        functools.partial(on_device, merged), mesh=mesh, in_specs=in_specs, out_specs=out_specs, check_vma=False
    )
```

```python
import functools

import jax
import jax.numpy as jnp
import numpy as np
from jax import lax
from jax.experimental import pallas as pl
from jax.experimental.pallas import tpu as pltpu
from jax.sharding import PartitionSpec as P

TILE = 128
NODE_DEV = 512
CELL_DEV = 8
core_radius = 0.1
shear_scale = 0.25
neighbour_offsets = ((-1, -1), (-1, 0), (-1, 1), (0, -1), (0, 1), (1, -1), (1, 0), (1, 1))
MONO = 35
MONO_PAD = 40
MOMENT_LANES = 384
UNROLL = 8
NODE_LOW = 256
f32 = jnp.float32
bf16 = jnp.bfloat16


def passed_along(block, axis, distance):
    size = lax.axis_size(axis)
    route = [((i - distance) % size, i) for i in range(size)]
    return lax.ppermute(block, axis, route)


PLAN = ((0, 1, 2, 5, 6, 7), (4,), (3,))


def exponent_table():
    rows = []
    for degree in range(5):
        for first in range(degree, -1, -1):
            for second in range(degree - first, -1, -1):
                rows.append((first, second, degree - first - second))
    table = np.zeros((3, MONO_PAD, TILE), np.float32)
    table[:, :MONO] = np.array(rows, np.float32).T[:, :, None]
    return table


def nt_dot(left, right):
    return lax.dot_general(left, right, (((1,), (1,)), ((), ())), preferred_element_type=f32)


def two_pieces(value):
    high = value.astype(bf16)
    return high, (value - high.astype(f32)).astype(bf16)


def cross(b, l):
    return [b[1] * l[2] - b[2] * l[1], b[2] * l[0] - b[0] * l[2], b[0] * l[1] - b[1] * l[0]]


def pack_kernel(*refs):
    (ghost_list, ghost_count), arrays = refs[:2], refs[2:10]
    packets, copies, (lists, counts, sems) = refs[10:-11], refs[-11:-3], refs[-3:]
    started = [pltpu.make_async_copy(ghost_list, lists, sems.at[8])]
    started += [pltpu.make_async_copy(ghost_count, counts, sems.at[9])]
    started += [pltpu.make_async_copy(a, b, sems.at[k]) for k, (a, b) in enumerate(zip(arrays, copies))]
    for copy in started:
        copy.start()
    for copy in started:
        copy.wait()
    mid, line, burgers = copies[:3]
    slots = lists.shape[0]
    for out, held in zip(packets, PLAN):
        for place, k in enumerate(held):
            for g in range(slots):
                valid = jnp.where(g < counts[0, k], 1.0, 0.0).astype(f32)
                at = pl.ds(lists[g, k], 1)
                rows = [mid[c, at] - 0.5 for c in range(3)]
                rows += cross([burgers[c, at] for c in range(3)], [line[c, at] for c in range(3)])
                packet = jnp.concatenate(rows + [jnp.zeros((2, TILE), f32)], axis=0) * valid
                out[place * slots + g] = packet


def moment_kernel(exponents, cell, mid, line, burgers, out, total):
    chunks = mid.shape[1] // 4
    total[...] = jnp.zeros(total.shape, f32)
    half = total.shape[0] // 2

    def step(i, carry):
        places = [pl.ds(4 * i + j, 1) for j in range(4)]
        wide = lambda ref, c: jnp.concatenate([ref[c, at] for at in places], axis=1)
        b, l = [wide(burgers, c) for c in range(3)], [wide(line, c) for c in range(3)]
        parts = []
        for at in places:
            value = None
            for c in range(3):
                base = 2.0 * (mid[c, at] - 0.5)
                powers = [base, base * base]
                powers += [powers[1] * base, powers[1] * powers[1]]
                power = jnp.ones((MONO_PAD, TILE), f32)
                for e in range(4):
                    power = jnp.where(exponents[c] == e + 1.0, powers[e], power)
                value = power if value is None else value * power
            parts.append(value)
        monomial = jnp.concatenate(parts, axis=1)
        rows = lax.broadcasted_iota(jnp.int32, (TILE, 4 * TILE), 0)
        cells = jnp.concatenate([cell[at] for at in places], axis=1)
        member = jnp.where(rows == cells, 1.0, 0.0).astype(bf16)
        terms = [monomial * (b[p // 3] * l[p % 3]) for p in range(9)]
        terms = jnp.concatenate(terms + [jnp.zeros((half - 9 * MONO_PAD, 4 * TILE), f32)], axis=0)
        total[...] += nt_dot(jnp.concatenate(two_pieces(terms), axis=0), member)
        return carry

    lax.fori_loop(0, chunks, step, 0)
    joined = total[:half] + total[half:]
    joined = [joined[p * MONO_PAD : p * MONO_PAD + MONO] for p in range(9)]
    joined = jnp.concatenate(joined + [jnp.zeros((MOMENT_LANES - 9 * MONO, TILE), f32)], axis=0)
    flipped = jnp.concatenate(
        [joined[k * TILE : (k + 1) * TILE].T for k in range(MOMENT_LANES // TILE)], axis=1
    )
    out[...] = flipped[: 9 * CELL_DEV].reshape(9, CELL_DEV, MOMENT_LANES)


def prepare_kernel(pair_list, pair_count, mid, items, spread):
    slots, _, tiles = pair_list.shape

    def listing(t, at):
        for n in range(slots):
            items[at + n + 1] = t * 64 + pair_list[n, 0, t]
        return at + pair_count[0, t]

    items[0] = lax.fori_loop(0, tiles, listing, 0, unroll=2)

    def widen(t, carry):
        rows = [mid[c, pl.ds(t, 1)] - 0.5 for c in range(3)]
        columns = jnp.concatenate(rows + [jnp.zeros((5, TILE), f32)], axis=0).T
        for c in range(3):
            spread[t, c] = jnp.broadcast_to(columns[:, c : c + 1], (TILE, TILE))
        return carry

    lax.fori_loop(0, tiles, widen, 0, unroll=4)


def write_features(source, features, s):
    y = [source[c, pl.ds(s, 1)] for c in range(3)]
    g = [shear_scale * source[c + 3, pl.ds(s, 1)] for c in range(3)]
    ys = [shear_scale * v for v in y]
    near = g + [2.0 * y[c] * g[c] for c in range(3)]
    near += [y[a] * g[b] + y[b] * g[a] for a, b in ((0, 1), (0, 2), (1, 2))]
    near = jnp.concatenate(near + [jnp.zeros((7, TILE), f32)], axis=0)
    far = [jnp.full((1, TILE), shear_scale, f32)] + ys
    far += [y[a] * ys[b] for a, b in ((0, 0), (1, 1), (2, 2), (0, 1), (0, 2), (1, 2))]
    far = jnp.concatenate(far + [jnp.zeros((6, TILE), f32)], axis=0)
    for base, value in ((0, near), (1, far)):
        high, low = two_pieces(value)
        rows, cols = base * 32, base * 2 * TILE
        features[s, rows : rows + 16, cols : cols + TILE] = high
        features[s, rows : rows + 16, cols + TILE : cols + 2 * TILE] = high
        features[s, rows + 16 : rows + 32, cols : cols + TILE] = low
        features[s, rows + 16 : rows + 32, cols + TILE : cols + 2 * TILE] = low
        other = (1 - base) * 2 * TILE
        features[s, rows : rows + 32, other : other + 2 * TILE] = jnp.zeros((32, 2 * TILE), bf16)


def add_items(items, count, source, features, spread, acc):
    def step(i, carry):
        results = []
        for u in range(UNROLL):
            item = items[i * UNROLL + u + 1]
            t, s = lax.shift_right_logical(item, 6), item & 63
            y = [source[c, pl.ds(s, 1)] for c in range(6)]
            r = [spread[t, c] - y[c] for c in range(3)]
            radius_sq = r[0] * r[0] + r[1] * r[1] + (r[2] * r[2] + core_radius**2)
            inverse = lax.rsqrt(radius_sq)
            inverse_sq = inverse * inverse
            near = inverse_sq * inverse
            p = r[0] * y[3] + r[1] * y[4] + r[2] * y[5]
            far = near * inverse_sq * p
            left = jnp.concatenate([*two_pieces(near), *two_pieces(far)], axis=1)
            results.append((t, nt_dot(left, features[s])))
        for t, value in results:
            acc[t] += value
        return carry

    lax.fori_loop(0, (count + UNROLL - 1) // UNROLL, step, 0)


def tile_force(acc_tile, x, b, l):
    flipped = acc_tile.T
    near = flipped[0:16] + flipped[16:32]
    far = flipped[32:48] + flipped[48:64]
    row = lambda block, k: block[k : k + 1]
    g = [row(near, c) for c in range(3)]
    q0 = row(far, 0)
    q = [row(far, 1 + c) for c in range(3)]
    trace = 0.5 * (row(near, 3) + row(near, 4) + row(near, 5))
    diagonal = x[0] * g[0] + x[1] * g[1] + x[2] * g[2] - trace + 1.5 * core_radius**2 * q0
    s = []
    for k, (m, n) in enumerate(((0, 0), (1, 1), (2, 2), (0, 1), (0, 2), (1, 2))):
        value = x[m] * g[n] + x[n] * g[m] - row(near, 3 + k)
        second = x[m] * (x[n] * q0 - q[n]) - x[n] * q[m] + row(far, 4 + k)
        value = value - 3.0 * second
        s.append(value + diagonal if m == n else value)
    traction = [
        s[0] * b[0] + s[3] * b[1] + s[4] * b[2],
        s[3] * b[0] + s[1] * b[1] + s[5] * b[2],
        s[4] * b[0] + s[5] * b[1] + s[2] * b[2],
    ]
    return [
        0.5 * (traction[1] * l[2] - traction[2] * l[1]),
        0.5 * (traction[2] * l[0] - traction[0] * l[2]),
        0.5 * (traction[0] * l[1] - traction[1] * l[0]),
    ]


def pair_kernel(merged, slots, *refs):
    item_list, spread, mid, line, burgers, node, moments, x_in, below, above = refs[:10]
    outs, (items, source, features, acc, force, grid) = refs[10:-6], refs[-6:]
    tiles = mid.shape[1]
    pool = tiles + 8 * slots
    total = item_list[0]

    def copy_items(k, carry):
        for u in range(8):
            items[k * 8 + u + 1] = item_list[k * 8 + u + 1]
        return carry

    lax.fori_loop(0, (total + 7) // 8, copy_items, 0)
    for u in range(UNROLL):
        items[total + u + 1] = pool
    for c in range(3):
        source[c, 0:tiles] = mid[c] - 0.5
    product = cross([burgers[c] for c in range(3)], [line[c] for c in range(3)])
    for c in range(3):
        source[c + 3, 0:tiles] = product[c]
    for c in range(6):
        source[c, pool : pool + 1] = jnp.zeros((1, TILE), f32)
    groups = [(below, 1), (x_in, 4), (above, 1), (below, 0), (above, 0), (below, 2), (x_in, 1), (above, 2)]
    for q, (arrived, place) in enumerate(groups):
        shift = neighbour_offsets[q] + (0,) * 4
        for g in range(slots):
            at = tiles + q * slots + g
            for c in range(6):
                source[c, at : at + 1] = arrived[place * slots + g, c : c + 1] + float(shift[c])

    def prepare(s, carry):
        write_features(source, features, s)
        return carry

    lax.fori_loop(0, pool, prepare, 0, unroll=2)
    features[pool] = jnp.zeros(features.shape[1:], bf16)

    def clear(t, carry):
        acc[t] = jnp.zeros(acc.shape[1:], f32)
        return carry

    lax.fori_loop(0, tiles, clear, 0)
    add_items(items, total, source, features, spread, acc)

    def finish(t, carry):
        at = pl.ds(t, 1)
        pick = lambda ref: [ref[c, at] for c in range(3)]
        rows = tile_force(acc[t], pick(source), pick(burgers), pick(line))
        for c in range(3):
            force[c, at] = rows[c]
        return carry

    lax.fori_loop(0, tiles, finish, 0, unroll=4)
    chunk = 4 * TILE
    grid[...] = jnp.zeros(grid.shape, f32)

    def scatter(i, carry):
        pieces = []
        for c in range(3):
            rest = jnp.concatenate([force[c, pl.ds(4 * i + j, 1)] for j in range(4)], axis=1)
            for k in range(3):
                piece = rest.astype(bf16).astype(f32)
                pieces.append(piece)
                rest = rest - piece
        for end in range(2):
            index = node[end : end + 1, pl.ds(pl.multiple_of(i * chunk, chunk), chunk)]
            high, low = lax.shift_right_logical(index, 8), index & (NODE_LOW - 1)
            mask = lax.broadcasted_iota(jnp.int32, (32, chunk), 0) == high
            left = jnp.concatenate([jnp.where(mask, v, 0.0).astype(bf16) for v in pieces], axis=0)
            lows = lax.broadcasted_iota(jnp.int32, (NODE_LOW, chunk), 0)
            right = jnp.where(lows == low, 1.0, 0.0).astype(bf16)
            grid[...] += nt_dot(left, right)
        return carry

    lax.fori_loop(0, tiles // 4, scatter, 0)
    halves = NODE_DEV // NODE_LOW
    sums = []
    for c in range(3):
        base = c * 96
        sums.append(grid[base : base + 32] + grid[base + 32 : base + 64] + grid[base + 64 : base + 96])

    def part(d):
        blocks = []
        for h in range(halves):
            k = d * halves + h
            blocks.append(jnp.concatenate([sums[c][k : k + 1] for c in range(3)] + [jnp.zeros((5, NODE_LOW), f32)], axis=0))
        return jnp.concatenate([moments[d]] + blocks, axis=1)

    for b in range(3):
        low, middle, high = part(b), part(3 + b), part(6 + b)
        outs[0][b] = middle
        if merged:
            outs[1][b] = low + high
        else:
            outs[1][b] = high
            outs[2][b] = low


def finish_kernel(middle, first, second, node_force, cells):
    total = middle[1] + first[...] + second[...]
    cells[...] = total[:, : cells.shape[1]]
    for k in range(NODE_DEV // TILE):
        at = MOMENT_LANES + k * TILE
        node_force[:, k : k + 1] = total[:3, at : at + TILE].reshape(3, 1, TILE)


def on_device(merged, seg_mid, seg_line, seg_burgers, seg_cell, seg_node, ghost_list, ghost_count, pair_list, pair_count):
    tiles, slots = seg_mid.shape[-1] // TILE, ghost_list.shape[-1]
    mid, line, burgers = [v.reshape(3, tiles, TILE) for v in (seg_mid, seg_line, seg_burgers)]
    cell = seg_cell.reshape(tiles, TILE)
    exponents = jnp.asarray(exponent_table())
    inputs = (mid, line, burgers, cell, seg_node[0, 0], exponents)
    inputs += (pair_list[0].transpose(2, 0, 1), pair_count[0])
    pairs = pair_list.shape[-1]
    plain = pl.BlockSpec()
    vmem = pl.BlockSpec(memory_space=pltpu.VMEM)
    hbm = pl.BlockSpec(memory_space=pltpu.HBM)
    smem = pl.BlockSpec(memory_space=pltpu.SMEM)
    shape = jax.ShapeDtypeStruct
    params = pltpu.CompilerParams(vmem_limit_bytes=32 * 2**20)
    cost = lambda flops: pl.CostEstimate(flops=flops, transcendentals=0, bytes_accessed=0)
    lists, counts = ghost_list[0, 0].T, ghost_count[0]
    results = pl.pallas_call(
        pack_kernel,
        in_specs=[hbm] * 10,
        out_specs=[vmem] * (len(PLAN) + 8),
        out_shape=[shape((len(held) * slots, 8, TILE), f32) for held in PLAN]
        + [shape(v.shape, v.dtype) for v in inputs],
        scratch_shapes=[
            pltpu.SMEM(lists.shape, jnp.int32),
            pltpu.SMEM(counts.shape, jnp.int32),
            pltpu.SemaphoreType.DMA((10,)),
        ],
        compiler_params=params,
        name="pack",
    )(*[pltpu.with_memory_space_constraint(v, pltpu.HBM) for v in (lists, counts, *inputs)])
    out_x, out_up, out_down = results[:3]
    mid, line, burgers, cell, node, exponents, pair_rows, pair_limits = results[3:]
    if merged:
        x_in = passed_along(out_x, "dx", 1)
    else:
        x_in = jnp.concatenate(
            [passed_along(out_x[: 3 * slots], "dx", -1), passed_along(out_x[3 * slots :], "dx", 1)]
        )
    pick = lambda k: x_in[k * slots : (k + 1) * slots]
    below = passed_along(jnp.concatenate([out_up, pick(5), pick(2)]), "dy", 1)
    above = passed_along(jnp.concatenate([out_down, pick(3), pick(0)]), "dy", -1)
    moments = pl.pallas_call(
        moment_kernel,
        in_specs=[vmem] * 5,
        out_specs=vmem,
        out_shape=shape((9, CELL_DEV, MOMENT_LANES), f32),
        scratch_shapes=[pltpu.VMEM((736, TILE), f32)],
        compiler_params=params,
        cost_estimate=cost(3 * 10**9),
        name="moments",
    )(exponents, cell, mid, line, burgers)
    room = tiles * pairs + 16
    item_list, spread = pl.pallas_call(
        prepare_kernel,
        in_specs=[smem, smem, vmem],
        out_specs=[smem, vmem],
        out_shape=[shape((room,), jnp.int32), shape((tiles, 3, TILE, TILE), f32)],
        compiler_params=params,
        cost_estimate=cost(3 * 10**9),
        name="prepare",
    )(pair_rows, pair_limits, mid)
    width = MOMENT_LANES + NODE_DEV
    count = 2 if merged else 3
    pool = tiles + 8 * slots
    parts = pl.pallas_call(
        functools.partial(pair_kernel, merged, slots),
        in_specs=[smem] + [vmem] * 9,
        out_specs=[vmem] * count,
        out_shape=[shape((3, 8, width), f32)] * count,
        scratch_shapes=[
            pltpu.SMEM((room,), jnp.int32),
            pltpu.VMEM((6, pool + 1, TILE), f32),
            pltpu.VMEM((pool + 1, 64, 4 * TILE), bf16),
            pltpu.VMEM((tiles, TILE, 64), f32),
            pltpu.VMEM((3, tiles, TILE), f32),
            pltpu.VMEM((288, NODE_LOW), f32),
        ],
        compiler_params=params,
        cost_estimate=cost(10**10),
        name="pairs",
    )(item_list, spread, mid, line, burgers, node, moments, x_in, below, above)
    middle = parts[0] + passed_along(parts[1], "dx", 1)
    if not merged:
        middle = middle + passed_along(parts[2], "dx", -1)
    node_force, cells = pl.pallas_call(
        finish_kernel,
        in_specs=[vmem] * 3,
        out_specs=[plain] * 2,
        out_shape=[shape((3, NODE_DEV // TILE, TILE), f32), shape((CELL_DEV, 9 * MONO), f32)],
        compiler_params=params,
        name="finish",
    )(middle, passed_along(middle[2], "dy", 1), passed_along(middle[0], "dy", -1))
    return node_force.reshape(1, 1, 3, NODE_DEV), cells.T


def solution(mesh):
    in_specs = (
        P("dx", "dy", None, None),
        P("dx", "dy", None, None),
        P("dx", "dy", None, None),
        P("dx", "dy", None),
        P("dx", "dy", None, None),
        P("dx", "dy", None, None),
        P("dx", "dy", None),
        P("dx", "dy", None, None),
        P("dx", "dy", None),
    )
    out_specs = (P("dx", "dy", None, None), P(None, ("dx", "dy")))
    merged = mesh.shape["dx"] == 2
    return jax.shard_map(
        functools.partial(on_device, merged), mesh=mesh, in_specs=in_specs, out_specs=out_specs, check_vma=False
    )
```
